128 devices in a mesh: gx: 8 (over z, core), gy: 4 (over y), vec: 4 (over x).
Axes of the slice: x: 4, y: 4, z: 4, core: 2. Of those that a mesh axis runs over, the one named last changes fastest.
Arguments:
- field: float32 [2, 256, 512], P(None, 'gx', 'gy'), may hold values from -4 to 4
- tangents: float32 [1024, 2, 256, 512], P('vec', None, 'gx', 'gy'), as said below
Outputs:
- field_next: float32 [2, 256, 512], P(None, 'gx', 'gy')
- vectors_next: float32 [1024, 2, 256, 512], P('vec', None, 'gx', 'gy')
The draws below stay inside these ranges and needn't reach their ends.
Inputs may be any that keep to these rules, and one draw needn't show every extreme that they name: `tangents`: real values; no vector is a combination of others.
All inputs are finite; a program needn't handle non-finite values.
Results may differ from the reference program's by a relative error of at most 0.0003.
Values sent between devices are 32-bit elements; how exact they have to be, the bound alone decides.
No kernel may reach another device: no remote copies, remote signals or barrier semaphores. Data moves between devices by JAX's collectives and lax.ppermute only.
A program may use at most 128 MiB of HBM per device.

```python
import math
import jax
import jax.numpy as jnp
from jax import lax

VEC_DEV = 256
LX = 256
LY = 512
NVECS = 1024
NDIM = 262144
N_VEC = 4


def draw_tangents(key, part):
    key_base, key_rough = jax.random.split(key, 2)
    shape = (NVECS, 2, LX, LY)
    base = jax.random.normal(key_base, shape, jnp.float32)
    mixed = base + 0.2 * (jnp.roll(base, -1, axis=0) + jnp.roll(base, -(NVECS // 4 + 3), axis=0) + jnp.roll(base, -(NVECS // 2 + 5), axis=0) + jnp.roll(base, -(3 * NVECS // 4 + 7), axis=0))
    positions = jnp.arange(LX, dtype=jnp.float32) / LX
    trend = jnp.exp(math.log(3.0) * positions)[:, None]
    rough = jnp.exp(jax.random.uniform(key_rough, (LX, LY), jnp.float32, math.log(0.5), math.log(2.0)))
    return mixed * (rough * trend)[None, None]


def block_levels(key, shape, cuts, low, largest):
    level = 1.0
    for axis_at, blocks in cuts:
        draws = jax.random.uniform(jax.random.fold_in(jax.random.fold_in(key, 6), axis_at), (blocks,), jnp.float32, low / len(cuts), largest / len(cuts))
        level = level * jnp.repeat(jnp.exp(draws), shape[axis_at] // blocks).reshape((-1,) + (1,) * (len(shape) - 1 - axis_at))
    return level


def normal_values(key, dims, width, reach, shards=(), kind=jnp.bfloat16):
    gain = block_levels(key, dims, shards, -0.22, 0.18) if shards else 1.0
    entries = jax.random.normal(key, dims, jnp.float32) * width * gain
    return jnp.minimum(jnp.maximum(entries, -reach), reach).astype(kind)


def setup_inputs(seed: int = 0) -> dict:
    seeds = jax.random.split(jax.random.key(seed), 3)
    field = normal_values(seeds[0], (2, LX, LY), 1.0, 4.0, ((1, 8), (2, 4)), jnp.float32)
    tangents = draw_tangents(jax.random.fold_in(seeds[2], 71), 0)
    return dict(field=field, tangents=tangents)


time_step = 0.2
coupling = 1.0
kerr_gain = 1.0

def neighbours(padded):
    return padded[..., :-2, 1:-1] + padded[..., 2:, 1:-1] + padded[..., 1:-1, :-2] + padded[..., 1:-1, 2:]

def wrap_pad(values):
    widths = [(0, 0)] * (values.ndim - 2) + [(1, 1), (1, 1)]
    return jnp.pad(values, widths, mode='wrap')

def field_rate(padded):
    centre = padded[:, 1:-1, 1:-1]
    neighbour_sum = neighbours(padded)
    re_part, im_part = (centre[0], centre[1])
    density = re_part * re_part + im_part * im_part
    return jnp.stack([-coupling * neighbour_sum[1] - kerr_gain * density * im_part, coupling * neighbour_sum[0] + kerr_gain * density * re_part])

def tangent_rate(base, padded):
    re_part, im_part = (base[0], base[1])
    neighbour_sum = neighbours(padded)
    centre = padded[:, :, 1:-1, 1:-1]
    re_tan, im_tan = (centre[:, 0], centre[:, 1])
    cross_term = 2.0 * re_part * im_part
    weight_re = 3.0 * re_part * re_part + im_part * im_part
    weight_im = re_part * re_part + 3.0 * im_part * im_part
    rate_re = -coupling * neighbour_sum[:, 1] - kerr_gain * (cross_term * re_tan + weight_im * im_tan)
    rate_im = coupling * neighbour_sum[:, 0] + kerr_gain * (weight_re * re_tan + cross_term * im_tan)
    return jnp.stack([rate_re, rate_im], axis=1)

def reference(field, tangents):
    highest = lax.Precision.HIGHEST
    field_half = field + 0.5 * time_step * field_rate(wrap_pad(field))
    field_next = field + time_step * field_rate(wrap_pad(field_half))

    def step_block(block):
        midpoint = block + 0.5 * time_step * tangent_rate(field, wrap_pad(block))
        return block + time_step * tangent_rate(field_half, wrap_pad(midpoint))
    blocks = tangents.reshape(N_VEC, VEC_DEV, 2, LX, LY)
    stepped = lax.map(step_block, blocks).reshape(NVECS, 2, LX, LY)
    panel = stepped[:VEC_DEV]
    remaining = stepped[VEC_DEV:]
    gram = jnp.einsum('vcrs,wcrs->vw', panel, panel, precision=highest) / NDIM
    factor = jnp.linalg.cholesky(gram)
    identity_mat = jnp.eye(VEC_DEV, dtype=jnp.float32)
    inverse = jax.scipy.linalg.solve_triangular(factor, identity_mat, lower=True)
    orthonormal = jnp.einsum('vw,wcrs->vcrs', inverse, panel, precision=highest)
    coefficients = jnp.einsum('vcrs,wcrs->vw', orthonormal, remaining, precision=highest) / NDIM
    projected = remaining - jnp.einsum('vw,vcrs->wcrs', coefficients, orthonormal, precision=highest)
    return (field_next, jnp.concatenate([orthonormal, projected], axis=0))
```

```python
import functools

import jax
import jax.numpy as jnp
from jax import lax
from jax.experimental import pallas as pl
from jax.experimental.pallas import tpu as pltpu
from jax.sharding import PartitionSpec as P

time_step = 0.2
XY = ("gx", "gy")
VB = 16
HIGHEST = lax.Precision.HIGHEST
F32 = jnp.float32


def params(mib=48):
    return pltpu.CompilerParams(vmem_limit_bytes=mib << 20)


def shape(*dims):
    return jax.ShapeDtypeStruct(dims, F32)


def lanes(rows):
    return lax.broadcasted_iota(jnp.int32, (rows, 128), 1)


def put_edges(packed, value, slab, lane):
    first = value if slab == 0 else pltpu.roll(value, slab, 1)
    packed = jnp.where(lane == slab, first, packed)
    shift = (65 + slab) % 128
    last = value if shift == 0 else pltpu.roll(value, shift, 1)
    return jnp.where(lane == 64 + slab, last, packed)


def pack_kernel(x_ref, f_ref, t_ref, top_ref, bot_ref, col_ref, *, rows):
    slabs = 2 * rows
    lane = lanes(VB)
    is_field = pl.program_id(0) == pl.num_programs(0) - 1

    @pl.when(jnp.logical_not(is_field))
    def _():
        for s in range(slabs):
            t_ref[0, s] = x_ref[pl.ds(s, VB, stride=slabs), :]

    @pl.when(is_field)
    def _():
        first = lax.broadcasted_iota(jnp.int32, (VB, 128), 0) == 0
        for s in range(slabs):
            t_ref[0, s] = jnp.where(first, jnp.broadcast_to(f_ref[s : s + 1, :], (VB, 128)), 0.0)

    packed = jnp.zeros((VB, 128), F32)
    for s in range(slabs):
        packed = put_edges(packed, t_ref[0, s], s, lane)
    col_ref[0] = packed
    for part in range(2):
        top_ref[0, part] = t_ref[0, part * rows]
        bot_ref[0, part] = t_ref[0, part * rows + rows - 1]


def set_weights(w_ref, field_row, rows):
    is_field = pl.program_id(0) == pl.num_programs(0) - 1

    @pl.when(pl.program_id(0) == 0)
    def _():
        for r in range(rows):
            a, b = field_row(r), field_row(rows + r)
            w_ref[0, r : r + 1, :] = 2.0 * a * b
            w_ref[1, r : r + 1, :] = 3.0 * a * a + b * b
            w_ref[2, r : r + 1, :] = a * a + 3.0 * b * b

    @pl.when(is_field)
    def _():
        for r in range(rows):
            a, b = field_row(r), field_row(rows + r)
            density = a * a + b * b
            w_ref[0, r : r + 1, :] = jnp.zeros_like(density)
            w_ref[1, r : r + 1, :] = density
            w_ref[2, r : r + 1, :] = density


def advance(t_ref, base_ref, up_ref, dn_ref, lf_ref, rt_ref, w_ref, rows, step, emit):
    lane = lanes(VB)
    from_left, from_right = lf_ref[0], rt_ref[0]

    def around(part, r):
        s = part * rows + r
        x = t_ref[0, s]
        above = t_ref[0, s - 1] if r > 0 else up_ref[0, part]
        below = t_ref[0, s + 1] if r < rows - 1 else dn_ref[0, part]
        left = jnp.where(lane == 0, pltpu.roll(from_left, 64 - s, 1), pltpu.roll(x, 1, 1))
        right = jnp.where(lane == 127, pltpu.roll(from_right, 127 - s, 1), pltpu.roll(x, 127, 1))
        return x, (above + below) + (left + right)

    for r in range(rows):
        u, sum_u = around(0, r)
        v, sum_v = around(1, r)
        cross, w_re, w_im = (w_ref[k, r : r + 1, :] for k in range(3))
        rate_u = -sum_v - (cross * u + w_im * v)
        rate_v = sum_u + (w_re * u + cross * v)
        emit(r, base_ref[0, r] + step * rate_u)
        emit(rows + r, base_ref[0, rows + r] + step * rate_v)


def half_kernel(t_ref, up_ref, dn_ref, lf_ref, rt_ref, f_ref, o_ref, top_ref, bot_ref, col_ref, w_ref, *, rows):
    set_weights(w_ref, lambda s: f_ref[s : s + 1, :], rows)
    lane = lanes(VB)
    packed = [jnp.zeros((VB, 128), F32)]

    def emit(s, value):
        o_ref[0, s] = value
        packed[0] = put_edges(packed[0], value, s, lane)

    advance(t_ref, t_ref, up_ref, dn_ref, lf_ref, rt_ref, w_ref, rows, 0.5 * time_step, emit)
    col_ref[0] = packed[0]
    for part in range(2):
        top_ref[0, part] = o_ref[0, part * rows]
        bot_ref[0, part] = o_ref[0, part * rows + rows - 1]


def full_kernel(t_ref, m_ref, up_ref, dn_ref, lf_ref, rt_ref, f_ref, o_ref, fn_ref, w_ref, *, rows):
    set_weights(w_ref, lambda s: f_ref[0, s, 0:1, :], rows)

    def emit(s, value):
        o_ref[0, s] = value

    advance(m_ref, t_ref, up_ref, dn_ref, lf_ref, rt_ref, w_ref, rows, time_step, emit)

    @pl.when(pl.program_id(0) == pl.num_programs(0) - 1)
    def _():
        for s in range(2 * rows):
            fn_ref[s : s + 1, :] = o_ref[0, s, 0:1, :]


def rotate(x, axis, by):
    n = lax.axis_size(axis)
    return lax.ppermute(x, axis, [(i, (i + by) % n) for i in range(n)])


def halos(top, bot, col):
    return rotate(bot, "gx", 1), rotate(top, "gx", -1), rotate(col, "gy", 1), rotate(col, "gy", -1)


def step_all(field, tangents):
    vectors, _, rows, cols = tangents.shape
    slabs = 2 * rows
    chunks = vectors // VB
    grid = (chunks + 1,)
    flat = tangents.reshape(vectors * slabs, cols)
    f2 = field.reshape(slabs, cols)
    big = pl.BlockSpec((1, slabs, VB, cols), lambda i: (i, 0, 0, 0))
    row = pl.BlockSpec((1, 2, VB, cols), lambda i: (i, 0, 0, 0))
    col = pl.BlockSpec((1, VB, cols), lambda i: (i, 0, 0))
    whole = pl.BlockSpec((slabs, cols), lambda i: (0, 0))
    shapes = (
        shape(chunks + 1, slabs, VB, cols),
        shape(chunks + 1, 2, VB, cols),
        shape(chunks + 1, 2, VB, cols),
        shape(chunks + 1, VB, cols),
    )
    t, top, bot, packed = pl.pallas_call(
        functools.partial(pack_kernel, rows=rows),
        grid=grid,
        in_specs=[pl.BlockSpec((VB * slabs, cols), lambda i: (jnp.minimum(i, chunks - 1), 0)), whole],
        out_specs=[big, row, row, col],
        out_shape=shapes,
        compiler_params=params(),
        name="pack",
    )(flat, f2)
    weights = [pltpu.VMEM((3, rows, cols), F32)]
    mid, top, bot, packed = pl.pallas_call(
        functools.partial(half_kernel, rows=rows),
        grid=grid,
        in_specs=[big, row, row, col, col, whole],
        out_specs=[big, row, row, col],
        out_shape=shapes,
        scratch_shapes=weights,
        compiler_params=params(),
        name="half",
    )(t, *halos(top, bot, packed), f2)
    half_field = pl.BlockSpec((1, slabs, VB, cols), lambda i: (chunks, 0, 0, 0))
    stepped, field_next = pl.pallas_call(
        functools.partial(full_kernel, rows=rows),
        grid=grid,
        in_specs=[big, big, row, row, col, col, half_field],
        out_specs=[big, whole],
        out_shape=(shapes[0], shape(slabs, cols)),
        scratch_shapes=weights,
        compiler_params=params(),
        name="full",
    )(t, mid, *halos(top, bot, packed), mid)
    return stepped, field_next.reshape(field.shape)


LAG = 2
RUN = 1


def broadcast_panel(stepped, chunks):
    here = lax.axis_index("vec")
    count = lax.axis_size("vec")
    ways = ([(i, i + 1) for i in range(count - 1)], [(0, count - 1)] + [(i, i - 1) for i in range(count - 1, 1, -1)])
    half = chunks // 2
    runs = half // RUN
    got = ([], [])
    for s in range(runs + LAG * (count - 2)):
        for d, pairs in enumerate(ways):
            k = min(s, runs - 1)
            own = lax.slice_in_dim(stepped, d * half + k * RUN, d * half + (k + 1) * RUN, axis=0)
            send = own if s < LAG else jnp.where(here == 0, own, got[d][s - LAG])
            got[d].append(lax.ppermute(send, "vec", pairs))
    return got


def fetch_panel(v_ref, s_ref, got_refs, panel_ref, sem, chunks, count):
    half = chunks // 2
    runs = half // RUN
    v = v_ref[0]

    def each(fn):
        for at in range(count):

            @pl.when(v == at)
            def _(at=at):
                for d in range(2):
                    hop = at if d == 0 else (count - at) % count
                    for k in range(runs):
                        c = d * half + k * RUN
                        if at == 0:
                            src = s_ref.at[pl.ds(c, RUN)]
                        else:
                            src = got_refs[d * len(got_refs) // 2 + k + LAG * (hop - 1)]
                        fn(pltpu.make_async_copy(src, panel_ref.at[pl.ds(c, RUN)], sem))

    each(lambda copy: copy.start())
    each(lambda copy: copy.wait())


def pair(ref, q, rows):
    both = [ref[:, 2 * q + k].reshape(rows, 128) for k in range(2)]
    return jnp.concatenate(both, axis=1)


NT = (((1,), (1,)), ((), ()))
TN = (((0,), (0,)), ((), ()))
NN = (((1,), (0,)), ((), ()))


def dot(a, b, dims):
    return lax.dot_general(a, b, dims, precision=HIGHEST, preferred_element_type=F32)


def gram_kernel(a_ref, g_ref, *, rows, pairs):
    @pl.when(pl.program_id(0) == 0)
    def _():
        g_ref[...] = jnp.zeros_like(g_ref)

    acc = g_ref[...]
    for q in range(pairs):
        a = pair(a_ref, q, rows)
        acc = acc + dot(a, a, NT)
    g_ref[...] = acc


def cross_kernel(v_ref, s_ref, *rest, rows, pairs, chunks, count):
    got_refs, (x_ref, panel_ref, mine_ref, sem) = rest[:-4], rest[-4:]
    own = pltpu.make_async_copy(s_ref.at[pl.ds(0, chunks)], mine_ref, sem.at[1])
    own.start()
    fetch_panel(v_ref, s_ref, got_refs, panel_ref, sem.at[0], chunks, count)
    own.wait()
    x_ref[...] = jnp.zeros_like(x_ref)

    def body(q, _):
        x_ref[...] += dot(pair(panel_ref, q, rows), pair(mine_ref, q, rows), NT)
        return 0

    lax.fori_loop(0, pairs, body, 0)


def final_kernel(v_ref, m_ref, s_block, s_ref, *rest, rows, pairs, chunks, count):
    got_refs, (o_ref, panel_ref, sem) = rest[:-3], rest[-3:]

    @pl.when(pl.program_id(0) == 0)
    def _():
        fetch_panel(v_ref, s_ref, got_refs, panel_ref, sem, chunks, count)

    keep = (v_ref[0] != 0).astype(F32)
    m = m_ref[...]
    out = o_ref.reshape(rows * 2 * pairs, 128)
    for q in range(pairs):
        base = pl.program_id(0) * pairs
        r = dot(m, pair(panel_ref, base + q, rows), NN)
        for k in range(2):
            mine = s_block[:, 2 * q + k].reshape(rows, 128)
            out[pl.ds(2 * q + k, rows, stride=2 * pairs), :] = keep * mine + r[:, 128 * k : 128 * k + 128]


CB = 32


def invert_kernel(g_ref, o_ref, a_ref, *, n, total):
    a_ref[:, 0:n] = g_ref[...] * (1.0 / total)
    eye = lax.broadcasted_iota(jnp.int32, (n, n), 0) == lax.broadcasted_iota(jnp.int32, (n, n), 1)
    a_ref[:, n : 2 * n] = eye.astype(F32)
    sub = lax.broadcasted_iota(jnp.int32, (CB, 1), 0)

    def block(p, _):
        at = pl.multiple_of(p * CB, CB)
        w = a_ref[pl.ds(at, CB), :]
        diag = pltpu.roll(w[:, 0:n], lax.rem(n - at, n), 1)[:, 0:128]
        for j in range(CB):
            scale = lax.rsqrt(diag[j : j + 1, j : j + 1])
            column = diag[:, j : j + 1] * scale
            w_row = w[j : j + 1, :] * scale
            d_row = diag[j : j + 1, :] * scale
            factor = jnp.where(sub > j, column, 0.0)
            w = jnp.where(sub == j, w_row, w - factor * w_row)
            diag = jnp.where(sub == j, d_row, diag - factor * d_row)
        a_ref[pl.ds(at, CB), :] = w
        below = lax.broadcasted_iota(jnp.int32, (CB, n), 1) >= at + CB
        a_ref[...] -= dot(jnp.where(below, w[:, 0:n], 0.0), w, TN)
        return 0

    lax.fori_loop(0, n // CB, block, 0)
    o_ref[...] = a_ref[:, n : 2 * n]


def coef_kernel(v_ref, x_ref, i_ref, m_ref, *, total):
    inverse = i_ref[...]
    coefficients = dot(inverse, x_ref[...] * (1.0 / total), NN)
    projected = -dot(coefficients, inverse, TN)
    m_ref[...] = jnp.where(v_ref[0] == 0, inverse, projected)


def scatter_sum(x):
    n = lax.axis_size("gx") * lax.axis_size("gy")
    return lax.all_to_all(x.reshape(n, x.shape[0] // n, x.shape[1]), XY, 0, 0).sum(0)


def gather_rows(y):
    n = lax.axis_size("gx") * lax.axis_size("gy")
    all_of = lax.all_to_all(jnp.broadcast_to(y[None], (n,) + y.shape), XY, 0, 0)
    return all_of.reshape(n * y.shape[0], y.shape[1])


def from_first(y):
    here = lax.axis_index("vec")
    others = [lax.ppermute(y, "vec", [(0, k)]) for k in range(1, lax.axis_size("vec"))]
    return jnp.where(here == 0, y, sum(others[1:], others[0]))


def local(field, tangents):
    vectors, _, rows, cols = tangents.shape
    slabs = 2 * rows
    chunks = vectors // VB
    count = lax.axis_size("vec")
    total = slabs * cols * lax.axis_size("gx") * lax.axis_size("gy")
    where = lax.axis_index("vec").astype(jnp.int32).reshape(1)
    stepped, field_next = step_all(field, tangents)
    got = broadcast_panel(stepped, chunks)
    got = got[0] + got[1]
    square = shape(vectors, vectors)
    per = 8
    blocked = pl.BlockSpec((chunks, per, VB, cols), lambda i: (0, i, 0, 0))
    smem = pl.BlockSpec(memory_space=pltpu.SMEM)
    hbm = pl.BlockSpec(memory_space=pl.ANY)
    gram = pl.pallas_call(
        functools.partial(gram_kernel, rows=vectors, pairs=per // 2),
        grid=(slabs // per,),
        in_specs=[blocked],
        out_specs=pl.BlockSpec((vectors, vectors), lambda i: (0, 0)),
        out_shape=square,
        compiler_params=params(),
        name="gram",
    )(stepped)
    gram = gather_rows(from_first(scatter_sum(gram)))
    inverse = pl.pallas_call(
        functools.partial(invert_kernel, n=vectors, total=total),
        out_shape=square,
        scratch_shapes=[pltpu.VMEM((vectors, 2 * vectors), F32)],
        compiler_params=params(),
        name="invert",
    )(gram)
    panel = pltpu.VMEM((chunks, slabs, VB, cols), F32)
    cross = pl.pallas_call(
        functools.partial(cross_kernel, rows=vectors, pairs=slabs // 2, chunks=chunks, count=count),
        in_specs=[smem, hbm] + [hbm] * len(got),
        out_shape=square,
        scratch_shapes=[panel, panel, pltpu.SemaphoreType.DMA((2,))],
        compiler_params=params(),
        name="cross",
    )(where, stepped, *got)
    cross = gather_rows(scatter_sum(cross))
    m = pl.pallas_call(
        functools.partial(coef_kernel, total=total),
        in_specs=[smem, pl.BlockSpec(memory_space=pltpu.VMEM), pl.BlockSpec(memory_space=pltpu.VMEM)],
        out_shape=square,
        compiler_params=params(),
        name="coef",
    )(where, cross, inverse)
    out = pl.pallas_call(
        functools.partial(final_kernel, rows=vectors, pairs=per // 2, chunks=chunks, count=count),
        grid=(slabs // per,),
        in_specs=[smem, pl.BlockSpec((vectors, vectors), lambda i: (0, 0)), blocked, hbm] + [hbm] * len(got),
        out_specs=pl.BlockSpec((vectors, per, cols), lambda i: (0, i, 0)),
        out_shape=shape(vectors, slabs, cols),
        scratch_shapes=[panel, pltpu.SemaphoreType.DMA],
        compiler_params=params(),
        name="final",
    )(where, m, stepped, stepped, *got)
    return field_next, out.reshape(tangents.shape)


def solution(mesh):
    specs = (P(None, "gx", "gy"), P("vec", None, "gx", "gy"))
    return jax.shard_map(local, mesh=mesh, in_specs=specs, out_specs=specs, check_vma=False)
```

```python
import functools

import jax
import jax.numpy as jnp
from jax import lax
from jax.experimental import pallas as pl
from jax.experimental.pallas import tpu as pltpu
from jax.sharding import PartitionSpec as P


time_step = 0.2
XY = ("gx", "gy")
VB = 16
HIGHEST = lax.Precision.HIGHEST
F32 = jnp.float32


def params(mib=8):
    return pltpu.CompilerParams(vmem_limit_bytes=mib << 20)


def shape(*dims):
    return jax.ShapeDtypeStruct(dims, F32)


def on_chip(*dims):
    return pltpu.VMEM(dims, F32)


WHOLE = pl.BlockSpec(memory_space=pltpu.VMEM)
SMEM = pl.BlockSpec(memory_space=pltpu.SMEM)
ANYWHERE = pl.BlockSpec(memory_space=pltpu.HBM)


def off_chip(x):
    return pltpu.with_memory_space_constraint(x, pltpu.HBM)


def lanes(rows):
    return lax.broadcasted_iota(jnp.int32, (rows, 128), 1)


def put_edges(packed, value, slab, lane):
    return jnp.where(lax.shift_right_logical(lane, 1) == slab, pltpu.roll(value, 2 * slab + 1, 1), packed)


def edges(get, slabs, lane):
    packed = [jnp.zeros((VB, 128), F32) for _ in range(4)]
    for s in range(slabs):
        packed[s % 4] = put_edges(packed[s % 4], get(s), s, lane)
    return (packed[0] + packed[1]) + (packed[2] + packed[3])


def pack_kernel(x_ref, f_ref, t_ref, top_ref, bot_ref, col_ref, *, rows):
    slabs = 2 * rows
    lane = lanes(VB)
    c = pl.program_id(0)
    is_field = c == pl.num_programs(0) - 1

    @pl.when(jnp.logical_not(is_field))
    def _():
        for s in range(slabs):
            t_ref[c, s] = x_ref[pl.ds(s, VB, stride=slabs), :]

    @pl.when(is_field)
    def _():
        first = lax.broadcasted_iota(jnp.int32, (VB, 128), 0) == 0
        for s in range(slabs):
            t_ref[c, s] = jnp.where(first, jnp.broadcast_to(f_ref[s : s + 1, :], (VB, 128)), 0.0)

    col_ref[c] = edges(lambda s: t_ref[c, s], slabs, lane)
    for part in range(2):
        top_ref[c, part] = t_ref[c, part * rows]
        bot_ref[c, part] = t_ref[c, part * rows + rows - 1]


def set_weights(w_ref, field_row, rows, with_field):
    def row(r, _):
        a, b = field_row(r), field_row(rows + r)
        at = pl.ds(r, 1)
        w_ref[0, 0, at, :] = 2.0 * a * b
        w_ref[0, 1, at, :] = 3.0 * a * a + b * b
        w_ref[0, 2, at, :] = a * a + 3.0 * b * b
        if with_field:
            density = a * a + b * b
            w_ref[1, 0, at, :] = jnp.zeros_like(density)
            w_ref[1, 1, at, :] = density
            w_ref[1, 2, at, :] = density
        return 0

    lax.fori_loop(0, rows, row, 0, unroll=4)


def advance(c, t_ref, base_ref, up_ref, dn_ref, lf_ref, rt_ref, w_ref, kind, rows, step, emit):
    lane = lanes(VB)
    odd = lax.rem(lane, 2) == 1
    sides = jnp.where(odd, pltpu.roll(lf_ref[c], 1, 1), pltpu.roll(rt_ref[c], 127, 1))
    at_first, at_last = lane == 0, lane == 127

    def around(part, r):
        s = part * rows + r
        x = t_ref[c, s]
        above = t_ref[c, s - 1] if r > 0 else up_ref[c, part]
        below = t_ref[c, s + 1] if r < rows - 1 else dn_ref[c, part]
        side = pltpu.roll(sides, 127 - 2 * s, 1)
        left = jnp.where(at_first, side, pltpu.roll(x, 1, 1))
        right = jnp.where(at_last, side, pltpu.roll(x, 127, 1))
        return x, (above + below) + (left + right)

    for r in range(rows):
        u, sum_u = around(0, r)
        v, sum_v = around(1, r)
        cross, w_re, w_im = (w_ref[kind, k, r : r + 1, :] for k in range(3))
        rate_u = -sum_v - (cross * u + w_im * v)
        rate_v = sum_u + (w_re * u + cross * v)
        emit(r, base_ref[c, r] + step * rate_u)
        emit(rows + r, base_ref[c, rows + r] + step * rate_v)


def half_kernel(t_ref, up_ref, dn_ref, lf_ref, rt_ref, f_ref, o_ref, top_ref, bot_ref, col_ref, w_ref, *, rows):
    set_weights(w_ref, lambda s: f_ref[pl.ds(s, 1), :], rows, True)
    lane = lanes(VB)
    chunks = t_ref.shape[0] - 1

    def chunk(c, _):
        def emit(s, value):
            o_ref[c, s] = value

        kind = (c == chunks).astype(jnp.int32)
        advance(c, t_ref, t_ref, up_ref, dn_ref, lf_ref, rt_ref, w_ref, kind, rows, 0.5 * time_step, emit)
        return 0

    lax.fori_loop(0, chunks + 1, chunk, 0)

    def pack(c, _):
        col_ref[c] = edges(lambda s: o_ref[c, s], 2 * rows, lane)
        for part in range(2):
            top_ref[c, part] = o_ref[c, part * rows]
            bot_ref[c, part] = o_ref[c, part * rows + rows - 1]
        return 0

    lax.fori_loop(0, chunks + 1, pack, 0)


def full_kernel(t_ref, m_ref, up_ref, dn_ref, lf_ref, rt_ref, *rest, rows, pieces, is_field):
    outs, w_ref = rest[:-1], rest[-1]
    field_at = t_ref.shape[0] - 1
    set_weights(w_ref, lambda s: m_ref[field_at, pl.ds(s, 1), 0, :], rows, is_field)
    for c, out in zip(pieces, outs):

        def emit(s, value, out=out):
            if is_field:
                out[s : s + 1, :] = value[0:1, :]
            else:
                out[0, s] = value

        advance(c, m_ref, t_ref, up_ref, dn_ref, lf_ref, rt_ref, w_ref, int(is_field), rows, time_step, emit)


def rotate(x, axis, by):
    n = lax.axis_size(axis)
    return lax.ppermute(x, axis, [(i, (i + by) % n) for i in range(n)])


def halos(top, bot, col):
    return rotate(bot, "gx", 1), rotate(top, "gx", -1), rotate(col, "gy", 1), rotate(col, "gy", -1)


def step_all(field, tangents):
    vectors, _, rows, cols = tangents.shape
    slabs = 2 * rows
    chunks = vectors // VB
    grid = (chunks + 1,)
    flat = tangents.reshape(vectors * slabs, cols)
    f2 = field.reshape(slabs, cols)
    whole = pl.BlockSpec((slabs, cols), lambda i: (0, 0))
    shapes = (
        on_chip(chunks + 1, slabs, VB, cols),
        on_chip(chunks + 1, 2, VB, cols),
        on_chip(chunks + 1, 2, VB, cols),
        on_chip(chunks + 1, VB, cols),
    )
    t, top, bot, packed = pl.pallas_call(
        functools.partial(pack_kernel, rows=rows),
        grid=grid,
        in_specs=[pl.BlockSpec((VB * slabs, cols), lambda i: (jnp.minimum(i, chunks - 1), 0)), whole],
        out_specs=[WHOLE] * 4,
        out_shape=shapes,
        compiler_params=params(),
        name="pack",
    )(pltpu.with_memory_space_constraint(flat, pltpu.HBM), f2)
    weights = [pltpu.VMEM((2, 3, rows, cols), F32)]
    mid, top, bot, packed = pl.pallas_call(
        functools.partial(half_kernel, rows=rows),
        in_specs=[WHOLE] * 6,
        out_specs=[WHOLE] * 4,
        out_shape=shapes,
        scratch_shapes=weights,
        compiler_params=params(),
        name="half",
    )(t, *halos(top, bot, packed), f2)
    sides = halos(top, bot, packed)

    def full(pieces, is_field, out_shape):
        return pl.pallas_call(
            functools.partial(full_kernel, rows=rows, pieces=pieces, is_field=is_field),
            in_specs=[WHOLE] * 6,
            out_specs=[WHOLE] * len(pieces),
            out_shape=(out_shape,) * len(pieces),
            scratch_shapes=weights,
            compiler_params=params(),
            name="full",
        )(t, mid, *sides)

    half = chunks // 2
    two = [full((k, half + k), False, pltpu.HBM((1, slabs, VB, cols), F32)) for k in range(half)]
    (field_next,) = full((chunks,), True, shape(slabs, cols))
    stepped = [pair[0] for pair in two] + [pair[1] for pair in two]
    return stepped, field_next.reshape(field.shape)


LAG = 2


def choose_kernel(v_ref, own_ref, passed_ref, o_ref, sem):
    @pl.when(v_ref[0] == 0)
    def _():
        copy = pltpu.make_async_copy(own_ref, o_ref, sem)
        copy.start()
        copy.wait()

    @pl.when(v_ref[0] != 0)
    def _():
        copy = pltpu.make_async_copy(passed_ref, o_ref, sem)
        copy.start()
        copy.wait()


def choose(where, own, passed):
    return pl.pallas_call(
        choose_kernel,
        in_specs=[SMEM, ANYWHERE, ANYWHERE],
        out_specs=ANYWHERE,
        out_shape=shape(*own.shape),
        scratch_shapes=[pltpu.SemaphoreType.DMA],
        compiler_params=params(2),
        name="choose",
    )(where, off_chip(own), off_chip(passed))


def broadcast_panel(stepped, chunks, where):
    half = chunks // 2
    ways = (((0, 1), (3, 2), (2, 3)), ((0, 3), (1, 2), (2, 1)))
    got = [[], []]
    for step in range(half + 2 * LAG):
        pieces = []
        for way in range(2):
            own = stepped[way * half + min(step, half - 1)]
            if step < LAG:
                pieces.append(own)
            else:
                passed = got[1 - way][step - LAG]
                pieces.append(choose(where, own, passed) if step < half else passed)
        for way in range(2):
            pair = [hop for at, hop in enumerate(ways[way]) if at * LAG <= step < half + at * LAG]
            arrived = lax.ppermute(pieces[way], "vec", pair)
            got[way].append(arrived)
    return got


PARTS = 4
SLOTS = 3


def slot_of(part):
    return part % SLOTS if isinstance(part, int) else lax.rem(part, SLOTS)


def fetch_own(own_refs, own_ref, sems, part, act):
    depth = own_ref.shape[2]
    slot, at_slabs = slot_of(part), pl.ds(part * depth, depth)
    for c, own in enumerate(own_refs):
        act(pltpu.make_async_copy(own.at[0, at_slabs], own_ref.at[slot, c], sems.at[1, slot]))


def start(copy):
    copy.start()


def wait(copy):
    copy.wait()


def fetch_panel(v_ref, own_refs, got_refs, panel_ref, sems, count, part, act):
    half = len(own_refs) // 2
    depth = panel_ref.shape[2]
    slot, at_slabs = slot_of(part), pl.ds(part * depth, depth)
    for at in range(count):

        @pl.when(v_ref[0] == at)
        def _(at=at):
            for way in range(2):
                hop = (at if way == 0 else count - at) - 1
                for k in range(half):
                    c = way * half + k
                    src = own_refs[c] if at == 0 else got_refs[(way + hop) % 2 * (len(got_refs) // 2) + k + LAG * hop]
                    copy = pltpu.make_async_copy(src.at[0, at_slabs], panel_ref.at[slot, c], sems.at[0, slot])
                    act(copy)


def pair(ref, slot, q, rows):
    both = [ref[slot, :, 2 * q + k].reshape(rows, 128) for k in range(2)]
    return jnp.concatenate(both, axis=1)


def halves(x):
    high = x.astype(jnp.bfloat16)
    return high, (x - high.astype(F32)).astype(jnp.bfloat16)


def dot3(a, b, dims):
    def part(x, y):
        return lax.dot_general(x, y, dims, preferred_element_type=F32)

    return part(a[0], b[0]) + (part(a[0], b[1]) + part(a[1], b[0]))


NT = (((1,), (1,)), ((), ()))
TN = (((0,), (0,)), ((), ()))
NN = (((1,), (0,)), ((), ()))


def dot(a, b, dims):
    return lax.dot_general(a, b, dims, precision=HIGHEST, preferred_element_type=F32)


def each_part(fetch, work):
    for part in range(SLOTS - 1):
        fetch(part, start)
    for part in range(PARTS):
        if part + SLOTS - 1 < PARTS:
            fetch(part + SLOTS - 1, start)
        fetch(part, wait)
        work(part % SLOTS)


def gram_kernel(v_ref, *rest, rows, pairs):
    own_refs, (g_ref, own_ref, sems) = rest[:-3], rest[-3:]

    def work(slot):
        acc = g_ref[...]
        for q in range(pairs):
            a = halves(pair(own_ref, slot, q, rows))
            acc = acc + dot3(a, a, NT)
        g_ref[...] = acc

    @pl.when(v_ref[0] == 0)
    def _():
        g_ref[...] = jnp.zeros_like(g_ref)
        each_part(lambda part, act: fetch_own(own_refs, own_ref, sems, part, act), work)


def cross_kernel(v_ref, *rest, rows, pairs, chunks, count):
    refs, (x_ref, panel_ref, own_ref, sems) = rest[:-4], rest[-4:]
    own_refs, got_refs = refs[:chunks], refs[chunks:]

    def fetch(part, act):
        fetch_panel(v_ref, own_refs, got_refs, panel_ref, sems, count, part, act)
        fetch_own(own_refs, own_ref, sems, part, act)

    def work(slot):
        acc = x_ref[...]
        for q in range(pairs):
            acc = acc + dot3(halves(pair(panel_ref, slot, q, rows)), halves(pair(own_ref, slot, q, rows)), NT)
        x_ref[...] = acc

    @pl.when(v_ref[0] != 0)
    def _():
        x_ref[...] = jnp.zeros_like(x_ref)
        each_part(fetch, work)


def final_kernel(v_ref, m_ref, *rest, rows, pairs, chunks, count):
    refs, (o_ref, panel_ref, own_ref, sems) = rest[:-4], rest[-4:]
    own_refs, got_refs = refs[:chunks], refs[chunks:]
    step = pl.program_id(0)

    def fetch(part, act):
        fetch_panel(v_ref, own_refs, got_refs, panel_ref, sems, count, part, act)
        fetch_own(own_refs, own_ref, sems, part, act)

    @pl.when(step == 0)
    def _():
        for part in range(SLOTS - 1):
            fetch(part, start)

    @pl.when(step + SLOTS - 1 < PARTS)
    def _():
        fetch(step + SLOTS - 1, start)

    fetch(step, wait)
    keep = (v_ref[0] != 0).astype(F32)
    m = halves(m_ref[...])
    out = o_ref.reshape(rows * 2 * pairs, 128)
    slot = slot_of(step)
    for q in range(pairs):
        r = dot3(m, halves(pair(panel_ref, slot, q, rows)), NN)
        r = keep * pair(own_ref, slot, q, rows) + r
        for k in range(2):
            out[pl.ds(2 * q + k, rows, stride=2 * pairs), :] = r[:, 128 * k : 128 * k + 128]


CB = 32


def invert_kernel(v_ref, g_ref, o_ref, a_ref, *, n, total):
    @pl.when(v_ref[0] == 0)
    def _():
        invert(g_ref, o_ref, a_ref, n, total)


def invert(g_ref, o_ref, a_ref, n, total):
    a_ref[:, 0:n] = g_ref[...] * (1.0 / total)
    eye = lax.broadcasted_iota(jnp.int32, (n, n), 0) == lax.broadcasted_iota(jnp.int32, (n, n), 1)
    a_ref[:, n : 2 * n] = eye.astype(F32)
    sub = lax.broadcasted_iota(jnp.int32, (CB, 1), 0)

    def block(p, _):
        at = pl.multiple_of(p * CB, CB)
        w = a_ref[pl.ds(at, CB), :]
        diag = pltpu.roll(w[:, 0:n], lax.rem(n - at, n), 1)[:, 0:128]
        for j in range(CB):
            scale = lax.rsqrt(diag[j : j + 1, j : j + 1])
            column = diag[:, j : j + 1] * scale
            w_row = w[j : j + 1, :] * scale
            d_row = diag[j : j + 1, :] * scale
            factor = jnp.where(sub > j, column, 0.0)
            w = jnp.where(sub == j, w_row, w - factor * w_row)
            diag = jnp.where(sub == j, d_row, diag - factor * d_row)
        a_ref[pl.ds(at, CB), :] = w
        below = lax.broadcasted_iota(jnp.int32, (CB, n), 1) >= at + CB
        a_ref[...] -= dot(jnp.where(below, w[:, 0:n], 0.0), w, TN)
        return 0

    lax.fori_loop(0, n // CB, block, 0)
    o_ref[...] = a_ref[:, n : 2 * n]


def coef_kernel(v_ref, x_ref, i_ref, m_ref, *, total):
    inverse = i_ref[...]
    coefficients = dot(inverse, x_ref[...] * (1.0 / total), NN)
    projected = -dot(coefficients, inverse, TN)
    m_ref[...] = jnp.where(v_ref[0] == 0, inverse, projected)


def scatter_sum(x):
    n = lax.axis_size("gx") * lax.axis_size("gy")
    parts = lax.all_to_all(x.reshape(n, x.shape[0] // n, x.shape[1]), XY, 0, 0)
    return parts.sum(0)


def gather_rows(y):
    n = lax.axis_size("gx") * lax.axis_size("gy")
    y_all = jnp.broadcast_to(y[None], (n,) + y.shape)
    all_of = lax.all_to_all(y_all, XY, 0, 0)
    return all_of.reshape(n * y.shape[0], y.shape[1])


def from_first(y):
    here = lax.axis_index("vec")
    others = []
    for k in range(1, lax.axis_size("vec")):
        others.append(lax.ppermute(y, "vec", [(0, k)]))
    return jnp.where(here == 0, y, sum(others[1:], others[0]))


def local(field, tangents):
    vectors, _, rows, cols = tangents.shape
    slabs = 2 * rows
    chunks = vectors // VB
    count = lax.axis_size("vec")
    total = slabs * cols * lax.axis_size("gx") * lax.axis_size("gy")
    where = lax.axis_index("vec").astype(jnp.int32).reshape(1)
    stepped, field_next = step_all(field, tangents)
    got = broadcast_panel(stepped, chunks, where)
    got = got[0] + got[1]
    square = shape(vectors, vectors)
    per = slabs // PARTS
    buffer = pltpu.VMEM((SLOTS, chunks, per, VB, cols), F32)
    sems = pltpu.SemaphoreType.DMA((2, SLOTS))
    gram = pl.pallas_call(
        functools.partial(gram_kernel, rows=vectors, pairs=per // 2),
        in_specs=[SMEM] + [ANYWHERE] * chunks,
        out_specs=WHOLE,
        out_shape=square,
        scratch_shapes=[buffer, sems],
        compiler_params=params(10),
        name="gram",
    )(where, *map(off_chip, stepped))
    gram = gather_rows(scatter_sum(gram))
    inverse = pl.pallas_call(
        functools.partial(invert_kernel, n=vectors, total=total),
        in_specs=[SMEM, WHOLE],
        out_shape=square,
        scratch_shapes=[pltpu.VMEM((vectors, 2 * vectors), F32)],
        compiler_params=params(),
        name="invert",
    )(where, gram)
    inverse = from_first(inverse)
    cross = pl.pallas_call(
        functools.partial(cross_kernel, rows=vectors, pairs=per // 2, chunks=chunks, count=count),
        in_specs=[SMEM] + [ANYWHERE] * (chunks + len(got)),
        out_specs=WHOLE,
        out_shape=square,
        scratch_shapes=[buffer, buffer, sems],
        compiler_params=params(16),
        name="cross",
    )(where, *map(off_chip, stepped), *map(off_chip, got))
    cross = gather_rows(scatter_sum(cross))
    m = pl.pallas_call(
        functools.partial(coef_kernel, total=total),
        in_specs=[SMEM, WHOLE, WHOLE],
        out_shape=square,
        compiler_params=params(),
        name="coef",
    )(where, cross, inverse)
    out = pl.pallas_call(
        functools.partial(final_kernel, rows=vectors, pairs=per // 2, chunks=chunks, count=count),
        grid=(PARTS,),
        in_specs=[SMEM, WHOLE] + [ANYWHERE] * (chunks + len(got)),
        out_specs=pl.BlockSpec((vectors, per, cols), lambda i: (0, i, 0)),
        out_shape=shape(vectors, slabs, cols),
        scratch_shapes=[buffer, buffer, sems],
        compiler_params=params(20),
        name="final",
    )(where, m, *map(off_chip, stepped), *map(off_chip, got))
    return field_next, out.reshape(tangents.shape)


def solution(mesh):
    specs = (P(None, "gx", "gy"), P("vec", None, "gx", "gy"))
    return jax.shard_map(local, mesh=mesh, in_specs=specs, out_specs=specs, check_vma=False)
```
